32 devices in a mesh: groups: 2 (over x), ctx: 16 (over z, y, core).
Axes of the slice: x: 2, y: 2, z: 4, core: 2. Of those that a mesh axis runs over, the one named last changes fastest.
Arguments:
- tokens: bfloat16 [32, 8192], P('groups', 'ctx'), parts along dimension 0, may hold values from -6 to 6
- attn_gain: float32 [8192], replicated, may hold values from 0.1 to 1.9
- mlp_gain: float32 [8192], replicated, may hold values from 0.1 to 1.9
- q_weight: bfloat16 [8192, 8192], P(None, 'ctx'), may hold values from -0.0625 to 0.0625
- k_weight: bfloat16 [8192, 1024], P('ctx'), may hold values from -0.5 to 0.5
- v_weight: bfloat16 [8192, 1024], P('ctx'), may hold values from -0.0625 to 0.0625
- o_weight: bfloat16 [8192, 8192], P(None, 'ctx'), may hold values from -0.0625 to 0.0625
- gate_weight: bfloat16 [8192, 16384], P(None, 'ctx'), may hold values from -0.0625 to 0.0625
- up_weight: bfloat16 [8192, 16384], P(None, 'ctx'), may hold values from -0.0625 to 0.0625
- down_weight: bfloat16 [16384, 8192], P('ctx'), may hold values from -0.046875 to 0.046875
- prefix_keys: bfloat16 [8192, 1024], P(('groups', 'ctx')), parts along dimension 0, may hold values from -400 to 400
- prefix_values: bfloat16 [8192, 1024], P(('groups', 'ctx')), parts along dimension 0, may hold values from -36 to 36
- suffix_keys: bfloat16 [256, 16, 1024], P(('groups', 'ctx')), parts along dimension 0, may hold values from -18 to 18
- suffix_values: bfloat16 [256, 16, 1024], P(('groups', 'ctx')), parts along dimension 0, may hold values from -18 to 18
- suffix_lengths: int32 [32], P('groups'), parts along dimension 0, may hold values from 1 to 128, as said below
- suffix_table: int32 [32, 8], P(('groups', 'ctx')), parts along dimension 0, may hold values from 0 to 7, as said below
Outputs:
- layer_out: bfloat16 [32, 8192], P('groups', 'ctx'), parts along dimension 0
The draws below stay inside these ranges and needn't reach their ends.
There are 2 independent parts, one for each index of `groups`. The reference program is written for one: setup_inputs(seed, part) draws one part's arguments, and reference() takes and returns one part's arrays. A program takes and returns all parts, laid end to end along the dimension named above; an argument that names none is the same for every part. Nothing has to cross between parts.
Inputs may be any that keep to these rules, and one draw needn't show every extreme that they name: `suffix_lengths`: at most 128; some sample has exactly 128. `suffix_table`: in every aligned block of 1 row, the entries name each of 0 to 7 exactly once.
All inputs are finite; a program needn't handle non-finite values.
Results may differ from the reference program's by a relative error of at most 0.014.
The reference program's roundings to bfloat16 on the way (of `attn_normed`, `queries`, `fresh_keys`, `fresh_values`, `attention`, `mixed`, `mlp_normed` and `hidden`) count: a program that leaves them out, or rounds other values in their place, can miss the bound.
Values may be sent and summed in bfloat16 or wider, within the bound.
No kernel may reach another device: no remote copies, remote signals or barrier semaphores. Data moves between devices by JAX's collectives and lax.ppermute only.
A program may use at most 128 MiB of HBM per device.

```python
import math
import jax
import jax.numpy as jnp
from jax import lax

D = 8192
HEADS = 64
KV_HEADS = 8
HEAD_DIM = 128
FFW = 16384
S_DEV = 1
BLK = 16
MAXB = 8
QW = 8192
KVW = 1024
S = 16
PRE = 4096
POOL = 128


def draw_suffix_lengths(key, part):
    suffix_span = MAXB * BLK
    lengths = jax.random.randint(key, (S,), 1, suffix_span + 1, dtype=jnp.int32)
    chosen = jax.random.randint(jax.random.fold_in(key, 11), (), 0, S, dtype=jnp.int32)
    return lengths.at[chosen].set(suffix_span)


def draw_suffix_table(key, part):
    device_count = S // S_DEV
    device_keys = jax.random.split(key, device_count)
    orders = jax.vmap(lambda single: jax.random.permutation(single, S_DEV * MAXB))(device_keys)
    return orders.astype(jnp.int32).reshape(S, MAXB)


def draw_prefix_keys(key, part):
    key_width = KV_HEADS * HEAD_DIM
    base = jnp.clip(jax.random.normal(key, (PRE, key_width), jnp.float32), -6.0, 6.0)
    return base.astype(jnp.bfloat16)


def block_levels(own_key, dims, pieces, least, largest):
    def one(axis_at, blocks):
        steps = jax.random.uniform(jax.random.fold_in(jax.random.fold_in(own_key, 6), axis_at), (blocks,), jnp.float32, least / len(pieces), largest / len(pieces))
        return jnp.repeat(jnp.exp(steps), dims[axis_at] // blocks).reshape((-1,) + (1,) * (len(dims) - axis_at - 1))

    level = one(*pieces[0])
    for cut in pieces[1:]:
        level = level * one(*cut)
    return level


def normal_values(stream_key, extent, width, reach, pieces=(), kind=jnp.bfloat16):
    result = width * jax.random.normal(stream_key, extent, jnp.float32)
    if pieces:
        result = result * block_levels(stream_key, extent, pieces, -0.22, 0.18)
    return jnp.clip(result, -reach, reach).astype(kind)


def setup_inputs(seed: int = 0, part: int = 0) -> dict:
    keys = jax.random.split(jax.random.key(seed), 17)
    part_splits = jax.random.split(jax.random.fold_in(keys[16], part), 17)
    tokens = normal_values(part_splits[0], (S, D), 1.0, 6.0, ((1, 16),))
    attn_gain = jnp.clip(1.0 + 0.18 * jax.random.normal(keys[1], (D,), jnp.float32), 0.1, 1.9)
    mlp_gain = jnp.clip(1.0 + 0.18 * jax.random.normal(keys[2], (D,), jnp.float32), 0.1, 1.9)
    q_weight = normal_values(keys[3], (D, QW), D ** -0.5, 0.0625, ((1, 16),))
    k_weight = normal_values(keys[4], (D, KVW), (D // 64) ** -0.5, 0.5, ((0, 16),))
    v_weight = normal_values(keys[5], (D, KVW), D ** -0.5, 0.0625, ((0, 16),))
    o_weight = normal_values(keys[6], (QW, D), QW ** -0.5, 0.0625, ((1, 16),))
    gate_weight = normal_values(keys[7], (D, FFW), D ** -0.5, 0.0625, ((1, 16),))
    up_weight = normal_values(keys[8], (D, FFW), D ** -0.5, 0.0625, ((1, 16),))
    down_weight = normal_values(keys[9], (FFW, D), FFW ** -0.5, 0.046875, ((0, 16),))
    prefix_keys = draw_prefix_keys(jax.random.fold_in(jax.random.fold_in(keys[16], part), 71), part)
    prefix_values = normal_values(part_splits[11], (PRE, KVW), 6.0, 36.0, ((0, 16),))
    suffix_keys = normal_values(part_splits[12], (POOL, BLK, KVW), 3.0, 18.0, ((0, 16),))
    suffix_values = normal_values(part_splits[13], (POOL, BLK, KVW), 3.0, 18.0, ((0, 16),))
    suffix_lengths = draw_suffix_lengths(jax.random.fold_in(jax.random.fold_in(keys[16], part), 71), part)
    suffix_table = draw_suffix_table(jax.random.fold_in(jax.random.fold_in(keys[16], part), 71), part)
    return {"tokens": tokens, "attn_gain": attn_gain, "mlp_gain": mlp_gain, "q_weight": q_weight, "k_weight": k_weight, "v_weight": v_weight, "o_weight": o_weight, "gate_weight": gate_weight, "up_weight": up_weight, "down_weight": down_weight, "prefix_keys": prefix_keys, "prefix_values": prefix_values, "suffix_keys": suffix_keys, "suffix_values": suffix_values, "suffix_lengths": suffix_lengths, "suffix_table": suffix_table}


EPSILON = 1e-05
ROPE_BASE = 500000.0

def rms_rows(matrix, gain_vector):
    widened = matrix.astype(jnp.float32)
    mean_square = lax.optimization_barrier(jnp.mean(widened * widened, axis=-1, keepdims=True))
    return (widened * lax.rsqrt(mean_square + EPSILON) * gain_vector).astype(jnp.bfloat16)

def rotate(matrix, position, columns):
    pair_index = (columns % HEAD_DIM // 2).astype(jnp.float32)
    frequency = jnp.exp(pair_index * (-2.0 * math.log(ROPE_BASE) / HEAD_DIM))
    angles = position.astype(jnp.float32)[:, None] * frequency[None, :]
    cosine = jnp.cos(angles[:, 0::2])
    sine_part = jnp.sin(angles[:, 0::2])
    even_part = matrix[:, 0::2]
    odd_part = matrix[:, 1::2]
    rotated_even = even_part * cosine - odd_part * sine_part
    rotated_odd = even_part * sine_part + odd_part * cosine
    return jnp.stack([rotated_even, rotated_odd], axis=-1).reshape(matrix.shape)

def reference(tokens, attn_gain, mlp_gain, q_weight, k_weight, v_weight, o_weight, gate_weight, up_weight, down_weight, prefix_keys, prefix_values, suffix_keys, suffix_values, suffix_lengths, suffix_table):
    samples = tokens.shape[0]
    group_size = HEADS // KV_HEADS
    score_scale = 1.0 / math.sqrt(HEAD_DIM)
    position = PRE + suffix_lengths
    attn_normed = rms_rows(tokens, attn_gain)
    query_cols = jnp.arange(HEADS * HEAD_DIM, dtype=jnp.int32)
    key_cols = jnp.arange(KV_HEADS * HEAD_DIM, dtype=jnp.int32)
    queries = rotate(jnp.dot(attn_normed, q_weight, preferred_element_type=jnp.float32), position, query_cols).astype(jnp.bfloat16)
    fresh_keys = rotate(jnp.dot(attn_normed, k_weight, preferred_element_type=jnp.float32), position, key_cols).astype(jnp.bfloat16)
    fresh_values = jnp.dot(attn_normed, v_weight, preferred_element_type=jnp.float32).astype(jnp.bfloat16)
    query_heads = queries.reshape(samples, KV_HEADS, group_size, HEAD_DIM).astype(jnp.float32)
    grouped = query_heads.transpose(1, 0, 2, 3)
    head_keys = prefix_keys.reshape(PRE, KV_HEADS, HEAD_DIM).astype(jnp.float32).transpose(1, 0, 2)
    head_values = prefix_values.reshape(PRE, KV_HEADS, HEAD_DIM).astype(jnp.float32).transpose(1, 0, 2)

    def prefix_head(operands):
        query_block, key_block, value_block = operands
        scores = jnp.einsum('sgd,td->sgt', query_block, key_block) * score_scale
        peak_block = lax.optimization_barrier(jnp.max(scores, axis=-1))
        weights = jnp.exp(scores - peak_block[..., None])
        total_block = lax.optimization_barrier(jnp.sum(weights, axis=-1))
        rounded = lax.optimization_barrier(weights.astype(jnp.bfloat16)).astype(jnp.float32)
        summed = jnp.einsum('sgt,td->sgd', rounded, value_block)
        return (peak_block, total_block, summed)
    peak_heads, total_heads, sum_heads = lax.map(prefix_head, (grouped, head_keys, head_values))
    prefix_peak = peak_heads.transpose(1, 0, 2).reshape(samples, HEADS)
    prefix_total = total_heads.transpose(1, 0, 2).reshape(samples, HEADS)
    prefix_sum = sum_heads.transpose(1, 0, 2, 3).reshape(samples, HEADS, HEAD_DIM)
    owner_base = jnp.arange(samples, dtype=jnp.int32) // S_DEV * (S_DEV * MAXB)
    blocks = owner_base[:, None] + suffix_table
    suffix_span = MAXB * BLK
    owned_keys = suffix_keys[blocks].reshape(samples, suffix_span, KV_HEADS, HEAD_DIM)
    owned_values = suffix_values[blocks].reshape(samples, suffix_span, KV_HEADS, HEAD_DIM)
    every_key = jnp.concatenate([owned_keys, fresh_keys.reshape(samples, 1, KV_HEADS, HEAD_DIM)], axis=1).astype(jnp.float32)
    every_value = jnp.concatenate([owned_values, fresh_values.reshape(samples, 1, KV_HEADS, HEAD_DIM)], axis=1).astype(jnp.float32)
    slot_index = jnp.arange(suffix_span + 1, dtype=jnp.int32)
    live_mask = (slot_index[None, :] < suffix_lengths[:, None]) | (slot_index[None, :] == suffix_span)
    suffix_scores = jnp.einsum('sngd,sjnd->sngj', query_heads, every_key) * score_scale
    suffix_scores = jnp.where(live_mask[:, None, None, :], suffix_scores, -1e+30)
    suffix_peak = lax.optimization_barrier(jnp.max(suffix_scores, axis=-1))
    suffix_weights = jnp.exp(suffix_scores - suffix_peak[..., None])
    suffix_total = lax.optimization_barrier(jnp.sum(suffix_weights, axis=-1)).reshape(samples, HEADS)
    suffix_rounded = lax.optimization_barrier(suffix_weights.astype(jnp.bfloat16)).astype(jnp.float32)
    suffix_sum = jnp.einsum('sngj,sjnd->sngd', suffix_rounded, every_value).reshape(samples, HEADS, HEAD_DIM)
    suffix_peak = suffix_peak.reshape(samples, HEADS)
    peak_all = jnp.maximum(prefix_peak, suffix_peak)
    prefix_factor = jnp.exp(prefix_peak - peak_all)
    suffix_factor = jnp.exp(suffix_peak - peak_all)
    numerator = prefix_sum * prefix_factor[..., None] + suffix_sum * suffix_factor[..., None]
    denominator = prefix_total * prefix_factor + suffix_total * suffix_factor
    attention = (numerator / denominator[..., None]).reshape(samples, HEADS * HEAD_DIM).astype(jnp.bfloat16)
    mixed = (tokens.astype(jnp.float32) + jnp.dot(attention, o_weight, preferred_element_type=jnp.float32)).astype(jnp.bfloat16)
    mlp_normed = rms_rows(mixed, mlp_gain)
    gate_proj = jnp.dot(mlp_normed, gate_weight, preferred_element_type=jnp.float32)
    up_proj = jnp.dot(mlp_normed, up_weight, preferred_element_type=jnp.float32)
    hidden = (jax.nn.silu(gate_proj) * up_proj).astype(jnp.bfloat16)
    layer_out = mixed.astype(jnp.float32) + jnp.dot(hidden, down_weight, preferred_element_type=jnp.float32)
    return layer_out.astype(jnp.bfloat16)
```

```python
import math

import jax
import jax.numpy as jnp
from jax import lax
from jax.sharding import PartitionSpec as P

HEADS = 64
KV_HEADS = 8
HEAD_DIM = 128


EPSILON = 1e-05
ROPE_BASE = 500000.0


def rotate(matrix, position, columns):
    pair_index = (columns % HEAD_DIM // 2).astype(jnp.float32)
    frequency = jnp.exp(pair_index * (-2.0 * math.log(ROPE_BASE) / HEAD_DIM))
    angles = position.astype(jnp.float32)[:, None] * frequency[None, :]
    cosine = jnp.cos(angles[:, 0::2])
    sine_part = jnp.sin(angles[:, 0::2])
    even_part = matrix[:, 0::2]
    odd_part = matrix[:, 1::2]
    rotated_even = even_part * cosine - odd_part * sine_part
    rotated_odd = even_part * sine_part + odd_part * cosine
    return jnp.stack([rotated_even, rotated_odd], axis=-1).reshape(matrix.shape)


def exchange(blocks):
    return lax.all_to_all(blocks, "ctx", 0, 0, tiled=True)


def gather_blocks(block):
    devices = lax.axis_size("ctx")
    return exchange(jnp.broadcast_to(block[None], (devices,) + block.shape))


def split_pieces(value, count):
    pieces = []
    rest = value
    for _ in range(count):
        piece = lax.reduce_precision(rest, 8, 7)
        pieces.append(piece.astype(jnp.bfloat16))
        rest = rest - piece
    return pieces


def normalized(blocks, gain_vector):
    devices, samples, width = blocks.shape
    widened = blocks.astype(jnp.float32)
    mean_square = jnp.sum(widened * widened, axis=(0, 2), keepdims=True) / (devices * width)
    scaled = widened * lax.rsqrt(mean_square + EPSILON) * gain_vector.reshape(devices, 1, width)
    return scaled.astype(jnp.bfloat16)


def columns_dot(blocks, weight):
    devices, samples, width = blocks.shape
    rows = blocks.transpose(1, 0, 2).reshape(samples, devices * width)
    return jnp.dot(rows, weight, preferred_element_type=jnp.float32)


def body(
    tokens,
    attn_gain,
    mlp_gain,
    q_weight,
    k_weight,
    v_weight,
    o_weight,
    gate_weight,
    up_weight,
    down_weight,
    prefix_keys,
    prefix_values,
    suffix_keys,
    suffix_values,
    suffix_lengths,
    suffix_table,
):
    self_index = lax.axis_index("ctx")
    devices = lax.axis_size("ctx")
    samples, width = tokens.shape
    own_rows = suffix_table.shape[0]
    group_size = HEADS // KV_HEADS
    score_scale = 1.0 / math.sqrt(HEAD_DIM)
    prefix_rows = prefix_keys.shape[0]
    row_start = self_index * own_rows
    position = prefix_rows * devices + suffix_lengths
    own_position = lax.dynamic_slice_in_dim(position, row_start, own_rows, 0)
    own_lengths = lax.dynamic_slice_in_dim(suffix_lengths, row_start, own_rows, 0)
    attn_normed = normalized(gather_blocks(tokens), attn_gain)
    local_normed = lax.dynamic_index_in_dim(attn_normed, self_index, 0, keepdims=False)
    query_width = q_weight.shape[1]
    query_cols = self_index * query_width + jnp.arange(query_width, dtype=jnp.int32)
    query_part = rotate(columns_dot(attn_normed, q_weight), position, query_cols).astype(
        jnp.bfloat16
    )
    key_width = k_weight.shape[1]
    key_term = jnp.dot(local_normed, k_weight, preferred_element_type=jnp.float32)
    value_term = jnp.dot(local_normed, v_weight, preferred_element_type=jnp.float32)
    fresh_high, fresh_low = split_pieces(jnp.concatenate([key_term, value_term], axis=1), 2)
    fresh_part = jnp.concatenate([fresh_high, fresh_low], axis=1).reshape(devices, -1)
    payload = jnp.concatenate(
        [jnp.broadcast_to(query_part.reshape(1, -1), (devices, query_part.size)), fresh_part],
        axis=1,
    ).reshape(devices, -1, HEAD_DIM)
    received = exchange(payload).reshape(devices, -1)
    queries = received[:, : query_part.size].reshape(devices, samples, query_width)
    queries = queries.transpose(1, 0, 2).reshape(samples, devices * query_width)
    fresh = received[:, query_part.size :].astype(jnp.float32)
    fresh = jnp.sum(fresh, axis=0).reshape(own_rows, 2, 2 * key_width)
    fresh = fresh[:, 0] + fresh[:, 1]
    fresh_keys = rotate(
        fresh[:, :key_width], own_position, jnp.arange(key_width, dtype=jnp.int32)
    ).astype(jnp.bfloat16)
    fresh_values = fresh[:, key_width:].astype(jnp.bfloat16)
    query_heads = queries.reshape(samples, KV_HEADS, group_size, HEAD_DIM)
    head_keys = prefix_keys.reshape(prefix_rows, KV_HEADS, HEAD_DIM)
    head_values = prefix_values.reshape(prefix_rows, KV_HEADS, HEAD_DIM)
    scores = (
        jnp.einsum("sngd,tnd->sngt", query_heads, head_keys, preferred_element_type=jnp.float32)
        * score_scale
    )
    local_peak = jnp.max(scores, axis=-1)
    weights = jnp.exp(scores - local_peak[..., None])
    local_total = jnp.sum(weights, axis=-1).reshape(samples, HEADS)
    local_peak = local_peak.reshape(samples, HEADS)
    local_sum = jnp.einsum(
        "sngt,tnd->sngd",
        weights.astype(jnp.bfloat16),
        head_values,
        preferred_element_type=jnp.float32,
    ).reshape(samples, HEADS * HEAD_DIM)
    stats = jnp.concatenate(split_pieces(local_peak, 3) + split_pieces(local_total, 3), axis=1)
    parts = jnp.concatenate([local_sum.astype(jnp.bfloat16), stats], axis=1)
    parts = exchange(parts.reshape(devices, own_rows, -1)).astype(jnp.float32)
    every_sum = parts[:, :, : HEADS * HEAD_DIM].reshape(devices, own_rows, HEADS, HEAD_DIM)
    stats = parts[:, :, HEADS * HEAD_DIM :].reshape(devices, own_rows, 2, 3, HEADS)
    stats = (stats[:, :, :, 0] + stats[:, :, :, 1]) + stats[:, :, :, 2]
    every_peak = stats[:, :, 0]
    every_total = stats[:, :, 1]
    own_queries = lax.dynamic_slice_in_dim(query_heads, row_start, own_rows, 0)
    blocks, block_size = suffix_keys.shape[:2]
    table_places = suffix_table.shape[1]
    owned_keys = suffix_keys.reshape(blocks * block_size, KV_HEADS, HEAD_DIM)
    owned_values = suffix_values.reshape(blocks * block_size, KV_HEADS, HEAD_DIM)
    places = jnp.arange(table_places, dtype=jnp.int32)
    held = suffix_table[:, :, None] == jnp.arange(blocks, dtype=jnp.int32)
    limit = jnp.where(held, own_lengths[:, None, None] - places[:, None] * block_size, 0)
    limit = jnp.max(limit, axis=1)
    live_mask = jnp.arange(block_size, dtype=jnp.int32) < limit[:, :, None]
    live_mask = live_mask.reshape(own_rows, 1, 1, blocks * block_size)
    slot_scores = (
        jnp.einsum("sngd,jnd->sngj", own_queries, owned_keys, preferred_element_type=jnp.float32)
        * score_scale
    )
    slot_scores = jnp.where(live_mask, slot_scores, -1e30)
    fresh_scores = score_scale * jnp.sum(
        own_queries.astype(jnp.float32)
        * fresh_keys.astype(jnp.float32).reshape(own_rows, KV_HEADS, 1, HEAD_DIM),
        axis=-1,
    )
    suffix_peak = jnp.maximum(jnp.max(slot_scores, axis=-1), fresh_scores)
    slot_weights = jnp.exp(slot_scores - suffix_peak[..., None])
    fresh_weights = jnp.exp(fresh_scores - suffix_peak)
    suffix_total = (jnp.sum(slot_weights, axis=-1) + fresh_weights).reshape(own_rows, HEADS)
    suffix_sum = jnp.einsum(
        "sngj,jnd->sngd",
        slot_weights.astype(jnp.bfloat16),
        owned_values,
        preferred_element_type=jnp.float32,
    )
    suffix_sum = suffix_sum + lax.reduce_precision(fresh_weights, 8, 7)[
        ..., None
    ] * fresh_values.astype(jnp.float32).reshape(own_rows, KV_HEADS, 1, HEAD_DIM)
    suffix_sum = suffix_sum.reshape(own_rows, HEADS, HEAD_DIM)
    suffix_peak = suffix_peak.reshape(own_rows, HEADS)
    peak_all = jnp.maximum(jnp.max(every_peak, axis=0), suffix_peak)
    part_factor = jnp.exp(every_peak - peak_all)
    suffix_factor = jnp.exp(suffix_peak - peak_all)
    numerator = (
        jnp.sum(every_sum * part_factor[..., None], axis=0) + suffix_sum * suffix_factor[..., None]
    )
    denominator = jnp.sum(every_total * part_factor, axis=0) + suffix_total * suffix_factor
    attention = (
        (numerator / denominator[..., None])
        .reshape(own_rows * HEADS, HEAD_DIM)
        .astype(jnp.bfloat16)
    )
    attention = gather_blocks(attention).reshape(samples, HEADS * HEAD_DIM)
    attended = jnp.dot(attention, o_weight, preferred_element_type=jnp.float32)
    mixed_rows = (tokens.astype(jnp.float32) + attended).astype(jnp.bfloat16)
    mlp_normed = normalized(gather_blocks(mixed_rows), mlp_gain)
    mlp_normed = mlp_normed.transpose(1, 0, 2).reshape(samples, devices * width)
    gate_proj = jnp.dot(mlp_normed, gate_weight, preferred_element_type=jnp.float32)
    up_proj = jnp.dot(mlp_normed, up_weight, preferred_element_type=jnp.float32)
    hidden = (jax.nn.silu(gate_proj) * up_proj).astype(jnp.bfloat16)
    partial_value = jnp.dot(hidden, down_weight, preferred_element_type=jnp.float32)
    partial_value = partial_value.astype(jnp.bfloat16).reshape(samples, devices, width)
    shares = exchange(partial_value.transpose(1, 0, 2))
    shares = jnp.sum(shares.astype(jnp.float32), axis=0)
    return (mixed_rows.astype(jnp.float32) + shares).astype(jnp.bfloat16)


def solution(mesh):
    placed = (
        P("groups", "ctx"),
        P(),
        P(),
        P(None, "ctx"),
        P("ctx", None),
        P("ctx", None),
        P(None, "ctx"),
        P(None, "ctx"),
        P(None, "ctx"),
        P("ctx", None),
        P(("groups", "ctx"), None),
        P(("groups", "ctx"), None),
        P(("groups", "ctx"), None, None),
        P(("groups", "ctx"), None, None),
        P("groups"),
        P(("groups", "ctx"), None),
    )
    return jax.shard_map(
        body, mesh=mesh, in_specs=placed, out_specs=P("groups", "ctx"), check_vma=False
    )
```

```python
import functools
import math

import jax
import jax.numpy as jnp
import numpy as np
from jax import lax
from jax.experimental import pallas as pl
from jax.experimental.pallas import tpu as pltpu
from jax.sharding import PartitionSpec as P

HEADS = 64
KV_HEADS = 8
HEAD_DIM = 128


EPSILON = 1e-05
ROPE_BASE = 500000.0


def rotate(matrix, position, columns):
    pair_index = (columns % HEAD_DIM // 2).astype(jnp.float32)
    frequency = jnp.exp(pair_index * (-2.0 * math.log(ROPE_BASE) / HEAD_DIM))
    angles = position.astype(jnp.float32)[:, None] * frequency[None, :]
    cosine = jnp.cos(angles[:, 0::2])
    sine_part = jnp.sin(angles[:, 0::2])
    even_part = matrix[:, 0::2]
    odd_part = matrix[:, 1::2]
    rotated_even = even_part * cosine - odd_part * sine_part
    rotated_odd = even_part * sine_part + odd_part * cosine
    return jnp.stack([rotated_even, rotated_odd], axis=-1).reshape(matrix.shape)


def exchange(blocks):
    return lax.all_to_all(blocks, "ctx", 0, 0, tiled=True)


def gather_blocks(block):
    devices = lax.axis_size("ctx")
    return exchange(jnp.broadcast_to(block[None], (devices,) + block.shape))


def split_pieces(value, count):
    pieces = []
    rest = value
    for _ in range(count):
        piece = lax.reduce_precision(rest, 8, 7)
        pieces.append(piece.astype(jnp.bfloat16))
        rest = rest - piece
    return pieces


def normalized(blocks, gain_vector):
    devices, samples, width = blocks.shape
    widened = blocks.astype(jnp.float32)
    mean_square = jnp.sum(widened * widened, axis=(0, 2), keepdims=True) / (devices * width)
    scaled = widened * lax.rsqrt(mean_square + EPSILON) * gain_vector.reshape(devices, 1, width)
    return scaled.astype(jnp.bfloat16)


def columns_dot(blocks, weight):
    devices, samples, width = blocks.shape
    rows = blocks.transpose(1, 0, 2).reshape(samples, devices * width)
    return jnp.dot(rows, weight, preferred_element_type=jnp.float32)


def body(
    tokens,
    attn_gain,
    mlp_gain,
    q_weight,
    k_weight,
    v_weight,
    o_weight,
    gate_weight,
    up_weight,
    down_weight,
    prefix_keys,
    prefix_values,
    suffix_keys,
    suffix_values,
    suffix_lengths,
    suffix_table,
):
    self_index = lax.axis_index("ctx")
    devices = lax.axis_size("ctx")
    samples, width = tokens.shape
    own_rows = suffix_table.shape[0]
    group_size = HEADS // KV_HEADS
    score_scale = 1.0 / math.sqrt(HEAD_DIM)
    prefix_rows = prefix_keys.shape[0]
    row_start = self_index * own_rows
    position = prefix_rows * devices + suffix_lengths
    own_position = lax.dynamic_slice_in_dim(position, row_start, own_rows, 0)
    own_lengths = lax.dynamic_slice_in_dim(suffix_lengths, row_start, own_rows, 0)
    attn_normed = normalized(gather_blocks(tokens), attn_gain)
    local_normed = lax.dynamic_index_in_dim(attn_normed, self_index, 0, keepdims=False)
    query_width = q_weight.shape[1]
    query_cols = self_index * query_width + jnp.arange(query_width, dtype=jnp.int32)
    query_part = rotate(columns_dot(attn_normed, q_weight), position, query_cols).astype(
        jnp.bfloat16
    )
    key_width = k_weight.shape[1]
    key_term = jnp.dot(local_normed, k_weight, preferred_element_type=jnp.float32)
    value_term = jnp.dot(local_normed, v_weight, preferred_element_type=jnp.float32)
    fresh_high, fresh_low = split_pieces(jnp.concatenate([key_term, value_term], axis=1), 2)
    fresh_part = jnp.concatenate([fresh_high, fresh_low], axis=1).reshape(devices, -1)
    payload = jnp.concatenate(
        [jnp.broadcast_to(query_part.reshape(1, -1), (devices, query_part.size)), fresh_part],
        axis=1,
    ).reshape(devices, -1, HEAD_DIM)
    received = exchange(payload).reshape(devices, -1)
    queries = received[:, : query_part.size].reshape(devices, samples, query_width)
    queries = queries.transpose(1, 0, 2).reshape(samples, devices * query_width)
    fresh = received[:, query_part.size :].astype(jnp.float32)
    fresh = jnp.sum(fresh, axis=0).reshape(own_rows, 2, 2 * key_width)
    fresh = fresh[:, 0] + fresh[:, 1]
    fresh_keys = rotate(
        fresh[:, :key_width], own_position, jnp.arange(key_width, dtype=jnp.int32)
    ).astype(jnp.bfloat16)
    fresh_values = fresh[:, key_width:].astype(jnp.bfloat16)
    query_heads = queries.reshape(samples, KV_HEADS, group_size, HEAD_DIM)
    head_keys = prefix_keys.reshape(prefix_rows, KV_HEADS, HEAD_DIM)
    head_values = prefix_values.reshape(prefix_rows, KV_HEADS, HEAD_DIM)
    scores = (
        jnp.einsum("sngd,tnd->sngt", query_heads, head_keys, preferred_element_type=jnp.float32)
        * score_scale
    )
    local_peak = jnp.max(scores, axis=-1)
    weights = jnp.exp(scores - local_peak[..., None])
    local_total = jnp.sum(weights, axis=-1).reshape(samples, HEADS)
    local_peak = local_peak.reshape(samples, HEADS)
    local_sum = jnp.einsum(
        "sngt,tnd->sngd",
        weights.astype(jnp.bfloat16),
        head_values,
        preferred_element_type=jnp.float32,
    ).reshape(samples, HEADS * HEAD_DIM)
    stats = jnp.concatenate(split_pieces(local_peak, 3) + split_pieces(local_total, 3), axis=1)
    parts = jnp.concatenate([local_sum.astype(jnp.bfloat16), stats], axis=1)
    parts = exchange(parts.reshape(devices, own_rows, -1)).astype(jnp.float32)
    every_sum = parts[:, :, : HEADS * HEAD_DIM].reshape(devices, own_rows, HEADS, HEAD_DIM)
    stats = parts[:, :, HEADS * HEAD_DIM :].reshape(devices, own_rows, 2, 3, HEADS)
    stats = (stats[:, :, :, 0] + stats[:, :, :, 1]) + stats[:, :, :, 2]
    every_peak = stats[:, :, 0]
    every_total = stats[:, :, 1]
    own_queries = lax.dynamic_slice_in_dim(query_heads, row_start, own_rows, 0)
    blocks, block_size = suffix_keys.shape[:2]
    table_places = suffix_table.shape[1]
    owned_keys = suffix_keys.reshape(blocks * block_size, KV_HEADS, HEAD_DIM)
    owned_values = suffix_values.reshape(blocks * block_size, KV_HEADS, HEAD_DIM)
    places = jnp.arange(table_places, dtype=jnp.int32)
    held = suffix_table[:, :, None] == jnp.arange(blocks, dtype=jnp.int32)
    limit = jnp.where(held, own_lengths[:, None, None] - places[:, None] * block_size, 0)
    limit = jnp.max(limit, axis=1)
    live_mask = jnp.arange(block_size, dtype=jnp.int32) < limit[:, :, None]
    live_mask = live_mask.reshape(own_rows, 1, 1, blocks * block_size)
    slot_scores = (
        jnp.einsum("sngd,jnd->sngj", own_queries, owned_keys, preferred_element_type=jnp.float32)
        * score_scale
    )
    slot_scores = jnp.where(live_mask, slot_scores, -1e30)
    fresh_scores = score_scale * jnp.sum(
        own_queries.astype(jnp.float32)
        * fresh_keys.astype(jnp.float32).reshape(own_rows, KV_HEADS, 1, HEAD_DIM),
        axis=-1,
    )
    suffix_peak = jnp.maximum(jnp.max(slot_scores, axis=-1), fresh_scores)
    slot_weights = jnp.exp(slot_scores - suffix_peak[..., None])
    fresh_weights = jnp.exp(fresh_scores - suffix_peak)
    suffix_total = (jnp.sum(slot_weights, axis=-1) + fresh_weights).reshape(own_rows, HEADS)
    suffix_sum = jnp.einsum(
        "sngj,jnd->sngd",
        slot_weights.astype(jnp.bfloat16),
        owned_values,
        preferred_element_type=jnp.float32,
    )
    suffix_sum = suffix_sum + lax.reduce_precision(fresh_weights, 8, 7)[
        ..., None
    ] * fresh_values.astype(jnp.float32).reshape(own_rows, KV_HEADS, 1, HEAD_DIM)
    suffix_sum = suffix_sum.reshape(own_rows, HEADS, HEAD_DIM)
    suffix_peak = suffix_peak.reshape(own_rows, HEADS)
    peak_all = jnp.maximum(jnp.max(every_peak, axis=0), suffix_peak)
    part_factor = jnp.exp(every_peak - peak_all)
    suffix_factor = jnp.exp(suffix_peak - peak_all)
    numerator = (
        jnp.sum(every_sum * part_factor[..., None], axis=0) + suffix_sum * suffix_factor[..., None]
    )
    denominator = jnp.sum(every_total * part_factor, axis=0) + suffix_total * suffix_factor
    attention = (
        (numerator / denominator[..., None])
        .reshape(own_rows * HEADS, HEAD_DIM)
        .astype(jnp.bfloat16)
    )
    attention = gather_blocks(attention).reshape(samples, HEADS * HEAD_DIM)
    attended = jnp.dot(attention, o_weight, preferred_element_type=jnp.float32)
    mixed_rows = (tokens.astype(jnp.float32) + attended).astype(jnp.bfloat16)
    mlp_normed = normalized(gather_blocks(mixed_rows), mlp_gain)
    mlp_normed = mlp_normed.transpose(1, 0, 2).reshape(samples, devices * width)
    gate_proj = jnp.dot(mlp_normed, gate_weight, preferred_element_type=jnp.float32)
    up_proj = jnp.dot(mlp_normed, up_weight, preferred_element_type=jnp.float32)
    hidden = (jax.nn.silu(gate_proj) * up_proj).astype(jnp.bfloat16)
    partial_value = jnp.dot(hidden, down_weight, preferred_element_type=jnp.float32)
    partial_value = partial_value.astype(jnp.bfloat16).reshape(samples, devices, width)
    shares = exchange(partial_value.transpose(1, 0, 2))
    shares = jnp.sum(shares.astype(jnp.float32), axis=0)
    return (mixed_rows.astype(jnp.float32) + shares).astype(jnp.bfloat16)


VMEM = pltpu.VMEM
SMEM = pltpu.SMEM
KIB = 1024
PIECES = 3
STAT_ROWS = 8


def whole(space):
    return pl.BlockSpec(memory_space=space)


def small_params(mebibytes):
    return pltpu.CompilerParams(vmem_limit_bytes=mebibytes * KIB * KIB)


def angles_kernel(lengths_ref, frequency_ref, cosine_ref, sine_ref, *, prefix_tokens):
    row = lax.broadcasted_iota(jnp.int32, cosine_ref.shape, 0)
    position = jnp.zeros(cosine_ref.shape, jnp.int32)
    for sample in range(cosine_ref.shape[0]):
        position = jnp.where(row == sample, prefix_tokens + lengths_ref[sample], position)
    angles = position.astype(jnp.float32) * frequency_ref[...]
    cosine_ref[...] = jnp.cos(angles)
    sine_ref[...] = jnp.sin(angles)


def rotated(head, cosine, sine):
    lane = lax.broadcasted_iota(jnp.int32, head.shape, 1)
    ahead = pltpu.roll(head, HEAD_DIM - 1, 1)
    behind = pltpu.roll(head, 1, 1)
    return head * cosine + jnp.where(lane % 2 == 0, -ahead, behind) * sine


def row_scale(blocks_ref):
    devices, samples, width = blocks_ref.shape
    total = jnp.zeros((samples, width), jnp.float32)
    for block in range(devices):
        widened = blocks_ref[block].astype(jnp.float32)
        total = total + widened * widened
    mean_square = jnp.sum(total, axis=1, keepdims=True) / (devices * width)
    return lax.rsqrt(mean_square + EPSILON)


def normed_block(blocks_ref, gain_ref, scale, block):
    widened = blocks_ref[block].astype(jnp.float32)
    width = widened.shape[1]
    gain = gain_ref[pl.ds(block * width, width)].reshape(1, width)
    return (widened * scale * gain).astype(jnp.bfloat16)


def project_kernel(
    self_ref, blocks_ref, gain_ref, cosine_ref, sine_ref, q_ref, k_ref, v_ref,
    payload_ref, normed_ref, fresh_ref,
):
    devices, samples, width = blocks_ref.shape
    scale = row_scale(blocks_ref)
    query = jnp.zeros((samples, q_ref.shape[1]), jnp.float32)
    for block in range(devices):
        normed = normed_block(blocks_ref, gain_ref, scale, block)
        normed_ref[block] = normed
        query = query + jnp.dot(
            normed, q_ref[block * width : (block + 1) * width, :],
            preferred_element_type=jnp.float32,
        )
    own = normed_ref[self_ref[0]]
    row = 0
    for weight_ref in (k_ref, v_ref):
        term = jnp.dot(own, weight_ref[...], preferred_element_type=jnp.float32)
        for place in range(0, term.shape[1], HEAD_DIM):
            fresh_ref[:, row, :] = term[:, place : place + HEAD_DIM]
            row += 1
    cosine = cosine_ref[...]
    sine = sine_ref[...]
    heads = q_ref.shape[1] // HEAD_DIM
    for head in range(heads):
        turned = rotated(query[:, head * HEAD_DIM : (head + 1) * HEAD_DIM], cosine, sine)
        turned = turned.astype(jnp.bfloat16)
        for peer in range(devices):
            payload_ref[peer, head * samples : (head + 1) * samples, :] = turned
    base = heads * samples
    fresh = fresh_ref[...]
    high = fresh.astype(jnp.bfloat16)
    payload_ref[:, base : base + row, :] = high
    low = (fresh - high.astype(jnp.float32)).astype(jnp.bfloat16)
    payload_ref[:, base + row : base + 2 * row, :] = low


def product_nt(left, right):
    return lax.dot_general(
        left, right, (((1,), (1,)), ((), ())), preferred_element_type=jnp.float32
    )


def stat_tile(peak, total):
    rows = peak.shape[0]
    lane = lax.broadcasted_iota(jnp.int32, (rows, HEAD_DIM), 1)
    tile = jnp.zeros((rows, HEAD_DIM), jnp.float32)
    place = 0
    for value in (peak, total):
        rest = value
        for _ in range(PIECES):
            piece = rest.astype(jnp.bfloat16).astype(jnp.float32)
            tile = jnp.where(lane == place, piece, tile)
            rest = rest - piece
            place += 1
    return tile


def stats_in_lanes(tile):
    row = lax.broadcasted_iota(jnp.int32, (STAT_ROWS, HEAD_DIM), 0)
    lane = lax.broadcasted_iota(jnp.int32, (STAT_ROWS, HEAD_DIM), 1)
    pick = (row == lane).astype(jnp.float32).astype(jnp.bfloat16)
    return product_nt(pick, tile.astype(jnp.bfloat16))


def attend_kernel(
    self_ref, lengths_ref, table_ref, blocks_ref, cosine_ref, sine_ref, keys_ref, values_ref,
    slot_keys_ref, slot_values_ref, payload_ref, suffix_sum_ref, suffix_stat_ref,
    sum_ref, stat_ref,
):
    devices = blocks_ref.shape[0]
    samples = payload_ref.shape[0]
    per_peer = HEADS // devices
    group = HEADS // KV_HEADS
    peers = group // per_peer
    query_rows = per_peer * samples
    fresh_rows = 2 * KV_HEADS
    score_scale = 1.0 / math.sqrt(HEAD_DIM)
    self_index = self_ref[0]
    fresh = jnp.zeros((fresh_rows, HEAD_DIM), jnp.float32)
    fresh_low = jnp.zeros((fresh_rows, HEAD_DIM), jnp.float32)
    for peer in range(devices):
        high = blocks_ref[peer, query_rows : query_rows + fresh_rows, :]
        low = blocks_ref[peer, query_rows + fresh_rows : query_rows + 2 * fresh_rows, :]
        fresh = fresh + high.astype(jnp.float32)
        fresh_low = fresh_low + low.astype(jnp.float32)
    fresh = fresh + fresh_low
    fresh_keys = rotated(
        fresh[:KV_HEADS], cosine_ref[pl.ds(self_index, 1), :], sine_ref[pl.ds(self_index, 1), :]
    )
    fresh_keys = fresh_keys.astype(jnp.bfloat16).astype(jnp.float32)
    fresh_values = fresh[KV_HEADS:].astype(jnp.bfloat16).astype(jnp.float32)
    slots = slot_keys_ref.shape[0]
    places = table_ref.shape[1]
    block_size = slots // places
    slot = lax.broadcasted_iota(jnp.int32, (1, slots), 1)
    limit = jnp.zeros((1, slots), jnp.int32)
    length = lengths_ref[self_index]
    for place in range(places):
        limit = jnp.where(
            slot // block_size == table_ref[0, place], length - place * block_size, limit
        )
    live = slot % block_size < limit
    group_row = lax.broadcasted_iota(jnp.int32, (group, group * samples), 0)
    group_lane = lax.broadcasted_iota(jnp.int32, (group, group * samples), 1)
    pick = (group_lane == group_row * samples + self_index).astype(jnp.float32)
    pick = pick.astype(jnp.bfloat16)
    suffix_tiles = []
    for head in range(KV_HEADS):
        lanes = slice(head * HEAD_DIM, (head + 1) * HEAD_DIM)
        query = jnp.concatenate(
            [blocks_ref[head * peers + peer, 0:query_rows, :] for peer in range(peers)], axis=0
        )
        scores = product_nt(query, keys_ref[:, lanes]) * score_scale
        peak = jnp.max(scores, axis=1, keepdims=True)
        weights = jnp.exp(scores - peak)
        total = jnp.sum(weights, axis=1, keepdims=True)
        summed = jnp.dot(
            weights.astype(jnp.bfloat16), values_ref[:, lanes], preferred_element_type=jnp.float32
        )
        tile = stat_tile(peak, total)
        for member in range(group):
            rows = slice(member * samples, (member + 1) * samples)
            sum_ref[:, head * group + member, :] = summed[rows]
            stat_ref[:, head * group + member, :] = tile[rows]
        own = jnp.dot(pick, query, preferred_element_type=jnp.float32)
        slot_scores = product_nt(own.astype(jnp.bfloat16), slot_keys_ref[:, lanes]) * score_scale
        slot_scores = jnp.where(live, slot_scores, -1e30)
        fresh_score = (
            jnp.sum(own * fresh_keys[head : head + 1], axis=1, keepdims=True) * score_scale
        )
        slot_peak = jnp.maximum(jnp.max(slot_scores, axis=1, keepdims=True), fresh_score)
        slot_weights = jnp.exp(slot_scores - slot_peak)
        fresh_weight = jnp.exp(fresh_score - slot_peak)
        slot_total = jnp.sum(slot_weights, axis=1, keepdims=True) + fresh_weight
        slot_sum = jnp.dot(
            slot_weights.astype(jnp.bfloat16), slot_values_ref[:, lanes],
            preferred_element_type=jnp.float32,
        )
        rounded = fresh_weight.astype(jnp.bfloat16).astype(jnp.float32)
        suffix_sum_ref[head * group : (head + 1) * group, :] = (
            slot_sum + rounded * fresh_values[head : head + 1]
        )
        suffix_tiles.append(stat_tile(slot_peak, slot_total))
    suffix_stat_ref[...] = stats_in_lanes(jnp.concatenate(suffix_tiles, axis=0))
    payload_ref[:, 0:HEADS, :] = sum_ref[...].astype(jnp.bfloat16)
    for sample in range(samples):
        stats = stats_in_lanes(stat_ref[sample])
        payload_ref[sample, HEADS : HEADS + STAT_ROWS, 0:HEADS] = stats.astype(jnp.bfloat16)
        payload_ref[sample, HEADS : HEADS + STAT_ROWS, HEADS:HEAD_DIM] = jnp.zeros(
            (STAT_ROWS, HEAD_DIM - HEADS), jnp.bfloat16
        )


def merge_kernel(blocks_ref, suffix_sum_ref, suffix_stat_ref, payload_ref, stat_ref):
    devices = blocks_ref.shape[0]
    stat_ref[...] = blocks_ref[:, HEADS : HEADS + STAT_ROWS, :].astype(jnp.float32)
    peaks = (stat_ref[:, 0, :] + stat_ref[:, 1, :]) + stat_ref[:, 2, :]
    totals = (stat_ref[:, 3, :] + stat_ref[:, 4, :]) + stat_ref[:, 5, :]
    peaks = peaks[:, :HEADS]
    totals = totals[:, :HEADS]
    own = suffix_stat_ref[...]
    suffix_peak = (own[0:1] + own[1:2]) + own[2:3]
    suffix_total = (own[3:4] + own[4:5]) + own[5:6]
    peak_all = jnp.maximum(jnp.max(peaks, axis=0, keepdims=True), suffix_peak)
    factor = jnp.exp(peaks - peak_all)
    suffix_factor = jnp.exp(suffix_peak - peak_all)
    denominator = (
        jnp.sum(totals * factor, axis=0, keepdims=True) + suffix_total * suffix_factor
    )
    shares = jnp.concatenate(
        [factor / denominator, jnp.broadcast_to(suffix_factor / denominator, (8, HEADS))], axis=0
    )
    high = shares.astype(jnp.bfloat16).astype(jnp.float32)
    rest = shares - high
    middle = rest.astype(jnp.bfloat16).astype(jnp.float32)
    row = lax.broadcasted_iota(jnp.int32, (HEADS, HEADS), 0)
    lane = lax.broadcasted_iota(jnp.int32, (HEADS, HEADS), 1)
    unit = (row == lane).astype(jnp.float32).astype(jnp.bfloat16)
    columns = product_nt(unit, high.astype(jnp.bfloat16)) + product_nt(
        unit, middle.astype(jnp.bfloat16)
    )
    mixed = suffix_sum_ref[...] * columns[:, devices : devices + 1]
    for peer in range(devices):
        part = blocks_ref[peer, 0:HEADS, :].astype(jnp.float32)
        mixed = mixed + part * columns[:, peer : peer + 1]
    attention = mixed.astype(jnp.bfloat16)
    for peer in range(devices):
        payload_ref[peer] = attention


def output_kernel(attention_ref, tokens_ref, o_ref, mixed_ref, payload_ref, wide_ref):
    wide_ref[...] = attention_ref[...].astype(jnp.float32)
    attended = jnp.zeros(tokens_ref.shape, jnp.float32)
    for head in range(0, HEADS, 2):
        pair = jnp.concatenate([wide_ref[:, head, :], wide_ref[:, head + 1, :]], axis=1)
        attended = attended + jnp.dot(
            pair.astype(jnp.bfloat16), o_ref[head * HEAD_DIM : (head + 2) * HEAD_DIM, :],
            preferred_element_type=jnp.float32,
        )
    mixed = (tokens_ref[...].astype(jnp.float32) + attended).astype(jnp.bfloat16)
    mixed_ref[...] = mixed
    for peer in range(payload_ref.shape[0]):
        payload_ref[peer] = mixed


def feed_kernel(blocks_ref, gain_ref, gate_ref, up_ref, down_ref, payload_ref):
    devices, samples, width = blocks_ref.shape
    scale = row_scale(blocks_ref)
    hidden_width = gate_ref.shape[1]
    gate = jnp.zeros((samples, hidden_width), jnp.float32)
    up = jnp.zeros((samples, hidden_width), jnp.float32)
    for block in range(devices):
        normed = normed_block(blocks_ref, gain_ref, scale, block)
        rows = slice(block * width, (block + 1) * width)
        gate = gate + jnp.dot(normed, gate_ref[rows, :], preferred_element_type=jnp.float32)
        up = up + jnp.dot(normed, up_ref[rows, :], preferred_element_type=jnp.float32)
    hidden = (gate * (1.0 / (1.0 + jnp.exp(-gate))) * up).astype(jnp.bfloat16)
    for peer in range(devices):
        payload_ref[peer] = jnp.dot(
            hidden, down_ref[:, peer * width : (peer + 1) * width],
            preferred_element_type=jnp.float32,
        ).astype(jnp.bfloat16)


def kernel_body(
    tokens,
    attn_gain,
    mlp_gain,
    q_weight,
    k_weight,
    v_weight,
    o_weight,
    gate_weight,
    up_weight,
    down_weight,
    prefix_keys,
    prefix_values,
    suffix_keys,
    suffix_values,
    suffix_lengths,
    suffix_table,
):
    self_index = lax.axis_index("ctx")
    devices = lax.axis_size("ctx")
    samples, width = tokens.shape
    self_array = self_index.astype(jnp.int32).reshape(1)
    pair_index = np.arange(HEAD_DIM, dtype=np.int32) // 2
    frequency = np.exp(
        pair_index.astype(np.float32) * np.float32(-2.0 * math.log(ROPE_BASE) / HEAD_DIM)
    )
    cosine, sine = pl.pallas_call(
        functools.partial(angles_kernel, prefix_tokens=prefix_keys.shape[0] * devices),
        name="angles",
        cost_estimate=pl.CostEstimate(flops=40000000000, bytes_accessed=1000, transcendentals=0),
        out_shape=[jax.ShapeDtypeStruct((samples, HEAD_DIM), jnp.float32)] * 2,
        in_specs=[whole(SMEM), whole(VMEM)],
        out_specs=[whole(VMEM)] * 2,
        compiler_params=small_params(1),
    )(suffix_lengths, jnp.asarray(frequency).reshape(1, HEAD_DIM))
    slots = suffix_keys.shape[0] * suffix_keys.shape[1]
    slot_keys = suffix_keys.reshape(slots, -1)
    slot_values = suffix_values.reshape(slots, -1)

    sent = jnp.broadcast_to(tokens[None], (devices,) + tokens.shape)
    token_blocks = exchange(sent)
    fresh_rows = 4 * KV_HEADS
    query_rows = samples * (width // HEAD_DIM)
    sent = pl.pallas_call(
        project_kernel,
        name="project",
        cost_estimate=pl.CostEstimate(flops=40000000000, bytes_accessed=1000, transcendentals=0),
        out_shape=jax.ShapeDtypeStruct((devices, query_rows + fresh_rows, HEAD_DIM), jnp.bfloat16),
        in_specs=[whole(SMEM)] + [whole(VMEM)] * 7,
        out_specs=whole(VMEM),
        scratch_shapes=[
            VMEM((devices, samples, width), jnp.bfloat16),
            VMEM((samples, fresh_rows // 2, HEAD_DIM), jnp.float32),
        ],
        compiler_params=small_params(8),
    )(self_array, token_blocks, attn_gain, cosine, sine, q_weight, k_weight, v_weight)
    query_blocks = exchange(sent)
    sent, suffix_sum, suffix_stat = pl.pallas_call(
        attend_kernel,
        name="attend",
        cost_estimate=pl.CostEstimate(flops=40000000000, bytes_accessed=1000, transcendentals=0),
        out_shape=[
            jax.ShapeDtypeStruct((samples, HEADS + STAT_ROWS, HEAD_DIM), jnp.bfloat16),
            jax.ShapeDtypeStruct((HEADS, HEAD_DIM), jnp.float32),
            jax.ShapeDtypeStruct((STAT_ROWS, HEADS), jnp.float32),
        ],
        in_specs=[whole(SMEM)] * 3 + [whole(VMEM)] * 7,
        out_specs=[whole(VMEM)] * 3,
        scratch_shapes=[
            VMEM((samples, HEADS, HEAD_DIM), jnp.float32),
            VMEM((samples, HEADS, HEAD_DIM), jnp.float32),
        ],
        compiler_params=small_params(8),
    )(
        self_array, suffix_lengths, suffix_table, query_blocks, cosine, sine,
        prefix_keys, prefix_values, slot_keys, slot_values,
    )
    part_blocks = exchange(sent)
    sent = pl.pallas_call(
        merge_kernel,
        name="merge",
        cost_estimate=pl.CostEstimate(flops=40000000000, bytes_accessed=1000, transcendentals=0),
        out_shape=jax.ShapeDtypeStruct((devices, HEADS, HEAD_DIM), jnp.bfloat16),
        in_specs=[whole(VMEM)] * 3,
        out_specs=whole(VMEM),
        scratch_shapes=[VMEM((devices, STAT_ROWS, HEAD_DIM), jnp.float32)],
        compiler_params=small_params(4),
    )(part_blocks, suffix_sum, suffix_stat)
    attention = exchange(sent)
    mixed, sent = pl.pallas_call(
        output_kernel,
        name="output",
        cost_estimate=pl.CostEstimate(flops=40000000000, bytes_accessed=1000, transcendentals=0),
        out_shape=[
            jax.ShapeDtypeStruct(tokens.shape, jnp.bfloat16),
            jax.ShapeDtypeStruct((devices,) + tokens.shape, jnp.bfloat16),
        ],
        in_specs=[whole(VMEM)] * 3,
        out_specs=[whole(VMEM)] * 2,
        scratch_shapes=[VMEM((samples, HEADS, HEAD_DIM), jnp.float32)],
        compiler_params=small_params(4),
    )(attention, tokens, o_weight)
    mixed_blocks = exchange(sent)
    sent = pl.pallas_call(
        feed_kernel,
        name="feed",
        cost_estimate=pl.CostEstimate(flops=1000, bytes_accessed=1000, transcendentals=0),
        out_shape=jax.ShapeDtypeStruct((devices,) + tokens.shape, jnp.bfloat16),
        in_specs=[whole(VMEM)] * 5,
        out_specs=whole(VMEM),
        compiler_params=small_params(4),
    )(mixed_blocks, mlp_gain, gate_weight, up_weight, down_weight)
    shares = jnp.sum(exchange(sent).astype(jnp.float32), axis=0)
    return (mixed.astype(jnp.float32) + shares).astype(jnp.bfloat16)


def fits_kernels(devices, args):
    tokens, k_weight, suffix_table = args[0], args[4], args[15]
    samples, width = tokens.shape
    return (
        width % HEAD_DIM == 0
        and HEADS % devices == 0
        and (HEADS // KV_HEADS) % (HEADS // devices) == 0
        and suffix_table.shape[0] == 1
        and samples == devices
        and samples % 16 == 0
        and k_weight.shape[0] == width
    )


def choose_body(*args):
    if fits_kernels(lax.axis_size("ctx"), args):
        return kernel_body(*args)
    return body(*args)


def solution(mesh):
    placed = (
        P("groups", "ctx"),
        P(),
        P(),
        P(None, "ctx"),
        P("ctx", None),
        P("ctx", None),
        P(None, "ctx"),
        P(None, "ctx"),
        P(None, "ctx"),
        P("ctx", None),
        P(("groups", "ctx"), None),
        P(("groups", "ctx"), None),
        P(("groups", "ctx"), None, None),
        P(("groups", "ctx"), None, None),
        P("groups"),
        P(("groups", "ctx"), None),
    )
    return jax.shard_map(
        choose_body, mesh=mesh, in_specs=placed, out_specs=P("groups", "ctx"), check_vma=False
    )
```

```python
import functools
import math

import jax
import jax.numpy as jnp
from jax import lax
from jax.experimental import pallas as pl
from jax.experimental.pallas import tpu as pltpu
from jax.sharding import PartitionSpec as P

HEADS = 64
KV_HEADS = 8
HEAD_DIM = 128


EPSILON = 1e-05
ROPE_BASE = 500000.0


def rotate(matrix, position, columns):
    pair_index = (columns % HEAD_DIM // 2).astype(jnp.float32)
    frequency = jnp.exp(pair_index * (-2.0 * math.log(ROPE_BASE) / HEAD_DIM))
    angles = position.astype(jnp.float32)[:, None] * frequency[None, :]
    cosine = jnp.cos(angles[:, 0::2])
    sine_part = jnp.sin(angles[:, 0::2])
    even_part = matrix[:, 0::2]
    odd_part = matrix[:, 1::2]
    rotated_even = even_part * cosine - odd_part * sine_part
    rotated_odd = even_part * sine_part + odd_part * cosine
    return jnp.stack([rotated_even, rotated_odd], axis=-1).reshape(matrix.shape)


def exchange(blocks):
    return lax.all_to_all(blocks, "ctx", 0, 0, tiled=True)


def gather_blocks(block):
    devices = lax.axis_size("ctx")
    return exchange(jnp.broadcast_to(block[None], (devices,) + block.shape))


def split_pieces(value, count):
    pieces = []
    rest = value
    for _ in range(count):
        piece = lax.reduce_precision(rest, 8, 7)
        pieces.append(piece.astype(jnp.bfloat16))
        rest = rest - piece
    return pieces


def normalized(blocks, gain_vector):
    devices, samples, width = blocks.shape
    widened = blocks.astype(jnp.float32)
    mean_square = jnp.sum(widened * widened, axis=(0, 2), keepdims=True) / (devices * width)
    scaled = widened * lax.rsqrt(mean_square + EPSILON) * gain_vector.reshape(devices, 1, width)
    return scaled.astype(jnp.bfloat16)


def columns_dot(blocks, weight):
    devices, samples, width = blocks.shape
    rows = blocks.transpose(1, 0, 2).reshape(samples, devices * width)
    return jnp.dot(rows, weight, preferred_element_type=jnp.float32)


def body(
    tokens,
    attn_gain,
    mlp_gain,
    q_weight,
    k_weight,
    v_weight,
    o_weight,
    gate_weight,
    up_weight,
    down_weight,
    prefix_keys,
    prefix_values,
    suffix_keys,
    suffix_values,
    suffix_lengths,
    suffix_table,
):
    self_index = lax.axis_index("ctx")
    devices = lax.axis_size("ctx")
    samples, width = tokens.shape
    own_rows = suffix_table.shape[0]
    group_size = HEADS // KV_HEADS
    score_scale = 1.0 / math.sqrt(HEAD_DIM)
    prefix_rows = prefix_keys.shape[0]
    row_start = self_index * own_rows
    position = prefix_rows * devices + suffix_lengths
    own_position = lax.dynamic_slice_in_dim(position, row_start, own_rows, 0)
    own_lengths = lax.dynamic_slice_in_dim(suffix_lengths, row_start, own_rows, 0)
    attn_normed = normalized(gather_blocks(tokens), attn_gain)
    local_normed = lax.dynamic_index_in_dim(attn_normed, self_index, 0, keepdims=False)
    query_width = q_weight.shape[1]
    query_cols = self_index * query_width + jnp.arange(query_width, dtype=jnp.int32)
    query_part = rotate(columns_dot(attn_normed, q_weight), position, query_cols).astype(
        jnp.bfloat16
    )
    key_width = k_weight.shape[1]
    key_term = jnp.dot(local_normed, k_weight, preferred_element_type=jnp.float32)
    value_term = jnp.dot(local_normed, v_weight, preferred_element_type=jnp.float32)
    fresh_high, fresh_low = split_pieces(jnp.concatenate([key_term, value_term], axis=1), 2)
    fresh_part = jnp.concatenate([fresh_high, fresh_low], axis=1).reshape(devices, -1)
    payload = jnp.concatenate(
        [jnp.broadcast_to(query_part.reshape(1, -1), (devices, query_part.size)), fresh_part],
        axis=1,
    ).reshape(devices, -1, HEAD_DIM)
    received = exchange(payload).reshape(devices, -1)
    queries = received[:, : query_part.size].reshape(devices, samples, query_width)
    queries = queries.transpose(1, 0, 2).reshape(samples, devices * query_width)
    fresh = received[:, query_part.size :].astype(jnp.float32)
    fresh = jnp.sum(fresh, axis=0).reshape(own_rows, 2, 2 * key_width)
    fresh = fresh[:, 0] + fresh[:, 1]
    fresh_keys = rotate(
        fresh[:, :key_width], own_position, jnp.arange(key_width, dtype=jnp.int32)
    ).astype(jnp.bfloat16)
    fresh_values = fresh[:, key_width:].astype(jnp.bfloat16)
    query_heads = queries.reshape(samples, KV_HEADS, group_size, HEAD_DIM)
    head_keys = prefix_keys.reshape(prefix_rows, KV_HEADS, HEAD_DIM)
    head_values = prefix_values.reshape(prefix_rows, KV_HEADS, HEAD_DIM)
    scores = (
        jnp.einsum("sngd,tnd->sngt", query_heads, head_keys, preferred_element_type=jnp.float32)
        * score_scale
    )
    local_peak = jnp.max(scores, axis=-1)
    weights = jnp.exp(scores - local_peak[..., None])
    local_total = jnp.sum(weights, axis=-1).reshape(samples, HEADS)
    local_peak = local_peak.reshape(samples, HEADS)
    local_sum = jnp.einsum(
        "sngt,tnd->sngd",
        weights.astype(jnp.bfloat16),
        head_values,
        preferred_element_type=jnp.float32,
    ).reshape(samples, HEADS * HEAD_DIM)
    stats = jnp.concatenate(split_pieces(local_peak, 3) + split_pieces(local_total, 3), axis=1)
    parts = jnp.concatenate([local_sum.astype(jnp.bfloat16), stats], axis=1)
    parts = exchange(parts.reshape(devices, own_rows, -1)).astype(jnp.float32)
    every_sum = parts[:, :, : HEADS * HEAD_DIM].reshape(devices, own_rows, HEADS, HEAD_DIM)
    stats = parts[:, :, HEADS * HEAD_DIM :].reshape(devices, own_rows, 2, 3, HEADS)
    stats = (stats[:, :, :, 0] + stats[:, :, :, 1]) + stats[:, :, :, 2]
    every_peak = stats[:, :, 0]
    every_total = stats[:, :, 1]
    own_queries = lax.dynamic_slice_in_dim(query_heads, row_start, own_rows, 0)
    blocks, block_size = suffix_keys.shape[:2]
    table_places = suffix_table.shape[1]
    owned_keys = suffix_keys.reshape(blocks * block_size, KV_HEADS, HEAD_DIM)
    owned_values = suffix_values.reshape(blocks * block_size, KV_HEADS, HEAD_DIM)
    places = jnp.arange(table_places, dtype=jnp.int32)
    held = suffix_table[:, :, None] == jnp.arange(blocks, dtype=jnp.int32)
    limit = jnp.where(held, own_lengths[:, None, None] - places[:, None] * block_size, 0)
    limit = jnp.max(limit, axis=1)
    live_mask = jnp.arange(block_size, dtype=jnp.int32) < limit[:, :, None]
    live_mask = live_mask.reshape(own_rows, 1, 1, blocks * block_size)
    slot_scores = (
        jnp.einsum("sngd,jnd->sngj", own_queries, owned_keys, preferred_element_type=jnp.float32)
        * score_scale
    )
    slot_scores = jnp.where(live_mask, slot_scores, -1e30)
    fresh_scores = score_scale * jnp.sum(
        own_queries.astype(jnp.float32)
        * fresh_keys.astype(jnp.float32).reshape(own_rows, KV_HEADS, 1, HEAD_DIM),
        axis=-1,
    )
    suffix_peak = jnp.maximum(jnp.max(slot_scores, axis=-1), fresh_scores)
    slot_weights = jnp.exp(slot_scores - suffix_peak[..., None])
    fresh_weights = jnp.exp(fresh_scores - suffix_peak)
    suffix_total = (jnp.sum(slot_weights, axis=-1) + fresh_weights).reshape(own_rows, HEADS)
    suffix_sum = jnp.einsum(
        "sngj,jnd->sngd",
        slot_weights.astype(jnp.bfloat16),
        owned_values,
        preferred_element_type=jnp.float32,
    )
    suffix_sum = suffix_sum + lax.reduce_precision(fresh_weights, 8, 7)[
        ..., None
    ] * fresh_values.astype(jnp.float32).reshape(own_rows, KV_HEADS, 1, HEAD_DIM)
    suffix_sum = suffix_sum.reshape(own_rows, HEADS, HEAD_DIM)
    suffix_peak = suffix_peak.reshape(own_rows, HEADS)
    peak_all = jnp.maximum(jnp.max(every_peak, axis=0), suffix_peak)
    part_factor = jnp.exp(every_peak - peak_all)
    suffix_factor = jnp.exp(suffix_peak - peak_all)
    numerator = (
        jnp.sum(every_sum * part_factor[..., None], axis=0) + suffix_sum * suffix_factor[..., None]
    )
    denominator = jnp.sum(every_total * part_factor, axis=0) + suffix_total * suffix_factor
    attention = (
        (numerator / denominator[..., None])
        .reshape(own_rows * HEADS, HEAD_DIM)
        .astype(jnp.bfloat16)
    )
    attention = gather_blocks(attention).reshape(samples, HEADS * HEAD_DIM)
    attended = jnp.dot(attention, o_weight, preferred_element_type=jnp.float32)
    mixed_rows = (tokens.astype(jnp.float32) + attended).astype(jnp.bfloat16)
    mlp_normed = normalized(gather_blocks(mixed_rows), mlp_gain)
    mlp_normed = mlp_normed.transpose(1, 0, 2).reshape(samples, devices * width)
    gate_proj = jnp.dot(mlp_normed, gate_weight, preferred_element_type=jnp.float32)
    up_proj = jnp.dot(mlp_normed, up_weight, preferred_element_type=jnp.float32)
    hidden = (jax.nn.silu(gate_proj) * up_proj).astype(jnp.bfloat16)
    partial_value = jnp.dot(hidden, down_weight, preferred_element_type=jnp.float32)
    partial_value = partial_value.astype(jnp.bfloat16).reshape(samples, devices, width)
    shares = exchange(partial_value.transpose(1, 0, 2))
    shares = jnp.sum(shares.astype(jnp.float32), axis=0)
    return (mixed_rows.astype(jnp.float32) + shares).astype(jnp.bfloat16)


VMEM = pltpu.VMEM
SMEM = pltpu.SMEM
KIB = 1024
PIECES = 3
STAT_ROWS = 8


def whole(space):
    return pl.BlockSpec(memory_space=space)


def small_params(mebibytes):
    return pltpu.CompilerParams(vmem_limit_bytes=mebibytes * KIB * KIB)


def exchange_like_cores(blocks):
    devices = lax.axis_size("ctx")
    sets = [[peer for peer in range(devices) if peer % 2 == core] for core in range(2)]
    return lax.all_to_all(blocks, "ctx", 0, 0, tiled=True, axis_index_groups=sets)


def swap_cores(blocks):
    devices = lax.axis_size("ctx")
    return lax.ppermute(blocks, "ctx", [(peer, peer ^ 1) for peer in range(devices)])


def gather_pairs(blocks):
    own = exchange_like_cores(blocks)
    return own, swap_cores(own)


def block_sources(own_ref, other_ref):
    core = lax.axis_index("ctx") % 2
    return [
        (source, pair, 2 * pair + (core if source is own_ref else 1 - core))
        for source in (own_ref, other_ref)
        for pair in range(own_ref.shape[0])
    ]


def spread_kernel(block_ref, payload_ref):
    for peer in range(payload_ref.shape[0]):
        payload_ref[peer] = block_ref[...]


def fill_angles(lengths_ref, prefix_tokens, cosine_ref, sine_ref):
    lane = lax.broadcasted_iota(jnp.int32, cosine_ref.shape, 1)
    frequency = jnp.exp(
        (lane // 2).astype(jnp.float32) * (-2.0 * math.log(ROPE_BASE) / HEAD_DIM)
    )
    row = lax.broadcasted_iota(jnp.int32, cosine_ref.shape, 0)
    position = jnp.zeros(cosine_ref.shape, jnp.int32)
    for sample in range(cosine_ref.shape[0]):
        position = jnp.where(row == sample, prefix_tokens + lengths_ref[sample], position)
    angles = position.astype(jnp.float32) * frequency
    cosine_ref[...] = jnp.cos(angles)
    sine_ref[...] = jnp.sin(angles)


def rotated(head, cosine, sine):
    lane = lax.broadcasted_iota(jnp.int32, head.shape, 1)
    ahead = pltpu.roll(head, HEAD_DIM - 1, 1)
    behind = pltpu.roll(head, 1, 1)
    return head * cosine + jnp.where(lane % 2 == 0, -ahead, behind) * sine


def row_scale(own_ref, other_ref):
    pairs, samples, width = own_ref.shape
    total = jnp.zeros((samples, width), jnp.float32)
    for source, pair, _ in block_sources(own_ref, other_ref):
        widened = source[pair].astype(jnp.float32)
        total = total + widened * widened
    mean_square = jnp.sum(total, axis=1, keepdims=True) / (2 * pairs * width)
    return lax.rsqrt(mean_square + EPSILON)


def normed_block(block, gain_ref, scale, place):
    widened = block.astype(jnp.float32)
    width = widened.shape[1]
    gain = gain_ref[pl.ds(pl.multiple_of(place * width, width), width)].reshape(1, width)
    return (widened * scale * gain).astype(jnp.bfloat16)


def project_kernel(
    lengths_ref, own_ref, other_ref, gain_ref, q_ref, k_ref, v_ref,
    payload_ref, cosine_ref, sine_ref, normed_ref, fresh_ref, *, prefix_tokens
):
    fill_angles(lengths_ref, prefix_tokens, cosine_ref, sine_ref)
    devices, samples, width = normed_ref.shape
    scale = row_scale(own_ref, other_ref)
    query = jnp.zeros((samples, q_ref.shape[1]), jnp.float32)
    for source, pair, place in block_sources(own_ref, other_ref):
        normed = normed_block(source[pair], gain_ref, scale, place)
        normed_ref[place] = normed
        rows = pl.ds(pl.multiple_of(place * width, width), width)
        query = query + jnp.dot(normed, q_ref[rows, :], preferred_element_type=jnp.float32)
    own = normed_ref[lax.axis_index("ctx")]
    row = 0
    for weight_ref in (k_ref, v_ref):
        term = jnp.dot(own, weight_ref[...], preferred_element_type=jnp.float32)
        for place in range(0, term.shape[1], HEAD_DIM):
            fresh_ref[:, row, :] = term[:, place : place + HEAD_DIM]
            row += 1
    cosine = cosine_ref[...]
    sine = sine_ref[...]
    heads = q_ref.shape[1] // HEAD_DIM
    for head in range(heads):
        turned = rotated(query[:, head * HEAD_DIM : (head + 1) * HEAD_DIM], cosine, sine)
        turned = turned.astype(jnp.bfloat16)
        for peer in range(devices):
            payload_ref[peer, head * samples : (head + 1) * samples, :] = turned
    base = heads * samples
    fresh = fresh_ref[...]
    high = fresh.astype(jnp.bfloat16)
    payload_ref[:, base : base + row, :] = high
    low = (fresh - high.astype(jnp.float32)).astype(jnp.bfloat16)
    payload_ref[:, base + row : base + 2 * row, :] = low


def product_nt(left, right):
    return lax.dot_general(
        left, right, (((1,), (1,)), ((), ())), preferred_element_type=jnp.float32
    )


def stat_tile(peak, total):
    rows = peak.shape[0]
    lane = lax.broadcasted_iota(jnp.int32, (rows, HEAD_DIM), 1)
    tile = jnp.zeros((rows, HEAD_DIM), jnp.float32)
    place = 0
    for value in (peak, total):
        rest = value
        for _ in range(PIECES):
            piece = rest.astype(jnp.bfloat16).astype(jnp.float32)
            tile = jnp.where(lane == place, piece, tile)
            rest = rest - piece
            place += 1
    return tile


def stats_in_lanes(tile):
    row = lax.broadcasted_iota(jnp.int32, (STAT_ROWS, HEAD_DIM), 0)
    lane = lax.broadcasted_iota(jnp.int32, (STAT_ROWS, HEAD_DIM), 1)
    pick = (row == lane).astype(jnp.float32).astype(jnp.bfloat16)
    return product_nt(pick, tile.astype(jnp.bfloat16))


def attend_kernel(
    lengths_ref, table_ref, blocks_ref, cosine_ref, sine_ref, keys_ref, values_ref,
    slot_keys_ref, slot_values_ref, payload_ref, suffix_sum_ref, suffix_stat_ref,
    sum_ref, stat_ref,
):
    devices = blocks_ref.shape[0]
    samples = payload_ref.shape[0]
    per_peer = HEADS // devices
    group = HEADS // KV_HEADS
    peers = group // per_peer
    query_rows = per_peer * samples
    fresh_rows = 2 * KV_HEADS
    score_scale = 1.0 / math.sqrt(HEAD_DIM)
    self_index = lax.axis_index("ctx")
    fresh = jnp.zeros((fresh_rows, HEAD_DIM), jnp.float32)
    fresh_low = jnp.zeros((fresh_rows, HEAD_DIM), jnp.float32)
    for peer in range(devices):
        high = blocks_ref[peer, query_rows : query_rows + fresh_rows, :]
        low = blocks_ref[peer, query_rows + fresh_rows : query_rows + 2 * fresh_rows, :]
        fresh = fresh + high.astype(jnp.float32)
        fresh_low = fresh_low + low.astype(jnp.float32)
    fresh = fresh + fresh_low
    fresh_keys = rotated(
        fresh[:KV_HEADS], cosine_ref[pl.ds(self_index, 1), :], sine_ref[pl.ds(self_index, 1), :]
    )
    fresh_keys = fresh_keys.astype(jnp.bfloat16).astype(jnp.float32)
    fresh_values = fresh[KV_HEADS:].astype(jnp.bfloat16).astype(jnp.float32)
    slots = slot_keys_ref.shape[0]
    places = table_ref.shape[1]
    block_size = slots // places
    slot = lax.broadcasted_iota(jnp.int32, (1, slots), 1)
    limit = jnp.zeros((1, slots), jnp.int32)
    length = lengths_ref[self_index]
    for place in range(places):
        limit = jnp.where(
            slot // block_size == table_ref[0, place], length - place * block_size, limit
        )
    live = slot % block_size < limit
    group_row = lax.broadcasted_iota(jnp.int32, (group, group * samples), 0)
    group_lane = lax.broadcasted_iota(jnp.int32, (group, group * samples), 1)
    pick = (group_lane == group_row * samples + self_index).astype(jnp.float32)
    pick = pick.astype(jnp.bfloat16)
    suffix_tiles = []
    for head in range(KV_HEADS):
        lanes = slice(head * HEAD_DIM, (head + 1) * HEAD_DIM)
        query = jnp.concatenate(
            [blocks_ref[head * peers + peer, 0:query_rows, :] for peer in range(peers)], axis=0
        )
        scores = product_nt(query, keys_ref[:, lanes]) * score_scale
        peak = jnp.max(scores, axis=1, keepdims=True)
        weights = jnp.exp(scores - peak)
        total = jnp.sum(weights, axis=1, keepdims=True)
        summed = jnp.dot(
            weights.astype(jnp.bfloat16), values_ref[:, lanes], preferred_element_type=jnp.float32
        )
        tile = stat_tile(peak, total)
        for member in range(group):
            rows = slice(member * samples, (member + 1) * samples)
            sum_ref[:, head * group + member, :] = summed[rows]
            stat_ref[:, head * group + member, :] = tile[rows]
        own = jnp.dot(pick, query, preferred_element_type=jnp.float32)
        slot_scores = product_nt(own.astype(jnp.bfloat16), slot_keys_ref[:, lanes]) * score_scale
        slot_scores = jnp.where(live, slot_scores, -1e30)
        fresh_score = (
            jnp.sum(own * fresh_keys[head : head + 1], axis=1, keepdims=True) * score_scale
        )
        slot_peak = jnp.maximum(jnp.max(slot_scores, axis=1, keepdims=True), fresh_score)
        slot_weights = jnp.exp(slot_scores - slot_peak)
        fresh_weight = jnp.exp(fresh_score - slot_peak)
        slot_total = jnp.sum(slot_weights, axis=1, keepdims=True) + fresh_weight
        slot_sum = jnp.dot(
            slot_weights.astype(jnp.bfloat16), slot_values_ref[:, lanes],
            preferred_element_type=jnp.float32,
        )
        rounded = fresh_weight.astype(jnp.bfloat16).astype(jnp.float32)
        suffix_sum_ref[head * group : (head + 1) * group, :] = (
            slot_sum + rounded * fresh_values[head : head + 1]
        )
        suffix_tiles.append(stat_tile(slot_peak, slot_total))
    suffix_stat_ref[...] = stats_in_lanes(jnp.concatenate(suffix_tiles, axis=0))
    payload_ref[:, 0:HEADS, :] = sum_ref[...].astype(jnp.bfloat16)
    for sample in range(samples):
        stats = stats_in_lanes(stat_ref[sample])
        payload_ref[sample, HEADS : HEADS + STAT_ROWS, 0:HEADS] = stats.astype(jnp.bfloat16)
        payload_ref[sample, HEADS : HEADS + STAT_ROWS, HEADS:HEAD_DIM] = jnp.zeros(
            (STAT_ROWS, HEAD_DIM - HEADS), jnp.bfloat16
        )


def merge_kernel(blocks_ref, suffix_sum_ref, suffix_stat_ref, payload_ref, stat_ref):
    devices = blocks_ref.shape[0]
    stat_ref[...] = blocks_ref[:, HEADS : HEADS + STAT_ROWS, :].astype(jnp.float32)
    peaks = (stat_ref[:, 0, :] + stat_ref[:, 1, :]) + stat_ref[:, 2, :]
    totals = (stat_ref[:, 3, :] + stat_ref[:, 4, :]) + stat_ref[:, 5, :]
    peaks = peaks[:, :HEADS]
    totals = totals[:, :HEADS]
    own = suffix_stat_ref[...]
    suffix_peak = (own[0:1] + own[1:2]) + own[2:3]
    suffix_total = (own[3:4] + own[4:5]) + own[5:6]
    peak_all = jnp.maximum(jnp.max(peaks, axis=0, keepdims=True), suffix_peak)
    factor = jnp.exp(peaks - peak_all)
    suffix_factor = jnp.exp(suffix_peak - peak_all)
    denominator = (
        jnp.sum(totals * factor, axis=0, keepdims=True) + suffix_total * suffix_factor
    )
    shares = jnp.concatenate(
        [factor / denominator, jnp.broadcast_to(suffix_factor / denominator, (8, HEADS))], axis=0
    )
    high = shares.astype(jnp.bfloat16).astype(jnp.float32)
    rest = shares - high
    middle = rest.astype(jnp.bfloat16).astype(jnp.float32)
    row = lax.broadcasted_iota(jnp.int32, (HEADS, HEADS), 0)
    lane = lax.broadcasted_iota(jnp.int32, (HEADS, HEADS), 1)
    unit = (row == lane).astype(jnp.float32).astype(jnp.bfloat16)
    columns = product_nt(unit, high.astype(jnp.bfloat16)) + product_nt(
        unit, middle.astype(jnp.bfloat16)
    )
    mixed = suffix_sum_ref[...] * columns[:, devices : devices + 1]
    for peer in range(devices):
        part = blocks_ref[peer, 0:HEADS, :].astype(jnp.float32)
        mixed = mixed + part * columns[:, peer : peer + 1]
    attention = mixed.astype(jnp.bfloat16)
    for peer in range(payload_ref.shape[0]):
        payload_ref[peer] = attention


def output_kernel(own_ref, other_ref, tokens_ref, o_ref, mixed_ref, wide_ref):
    for source, pair, place in block_sources(own_ref, other_ref):
        wide_ref[place] = source[pair].astype(jnp.float32)
    attended = jnp.zeros(tokens_ref.shape, jnp.float32)
    for head in range(0, HEADS, 2):
        pair = jnp.concatenate([wide_ref[:, head, :], wide_ref[:, head + 1, :]], axis=1)
        attended = attended + jnp.dot(
            pair.astype(jnp.bfloat16), o_ref[head * HEAD_DIM : (head + 2) * HEAD_DIM, :],
            preferred_element_type=jnp.float32,
        )
    mixed = (tokens_ref[...].astype(jnp.float32) + attended).astype(jnp.bfloat16)
    mixed_ref[...] = mixed


def feed_kernel(
    own_ref, other_ref, gain_ref, gate_ref, up_ref, down_ref, own_sums_ref, other_sums_ref
):
    pairs, samples, width = own_ref.shape
    core = lax.axis_index("ctx") % 2
    scale = row_scale(own_ref, other_ref)
    hidden_width = gate_ref.shape[1]
    gate = jnp.zeros((samples, hidden_width), jnp.float32)
    up = jnp.zeros((samples, hidden_width), jnp.float32)
    for source, pair, place in block_sources(own_ref, other_ref):
        normed = normed_block(source[pair], gain_ref, scale, place)
        rows = pl.ds(pl.multiple_of(place * width, width), width)
        gate = gate + jnp.dot(normed, gate_ref[rows, :], preferred_element_type=jnp.float32)
        up = up + jnp.dot(normed, up_ref[rows, :], preferred_element_type=jnp.float32)
    hidden = (gate * (1.0 / (1.0 + jnp.exp(-gate))) * up).astype(jnp.bfloat16)
    for side, sums_ref in enumerate((other_sums_ref, own_sums_ref)):
        for pair in range(pairs):
            place = 2 * pair + (1 - core if side == 0 else core)
            columns = pl.ds(pl.multiple_of(place * width, width), width)
            sums_ref[pair] = jnp.dot(
                hidden, down_ref[:, columns], preferred_element_type=jnp.float32
            ).astype(sums_ref.dtype)


def pair_kernel(own_sums_ref, received_ref, payload_ref):
    payload_ref[...] = (own_sums_ref[...] + received_ref[...].astype(jnp.float32)).astype(
        jnp.bfloat16
    )


def kernel_body(
    tokens,
    attn_gain,
    mlp_gain,
    q_weight,
    k_weight,
    v_weight,
    o_weight,
    gate_weight,
    up_weight,
    down_weight,
    prefix_keys,
    prefix_values,
    suffix_keys,
    suffix_values,
    suffix_lengths,
    suffix_table,
):
    devices = lax.axis_size("ctx")
    samples, width = tokens.shape
    def spread(name, block):
        return pl.pallas_call(
            spread_kernel,
            name=name,
            cost_estimate=pl.CostEstimate(flops=40000000000, bytes_accessed=1000, transcendentals=0),
            out_shape=jax.ShapeDtypeStruct((devices // 2,) + block.shape, block.dtype),
            in_specs=[whole(VMEM)],
            out_specs=whole(VMEM),
            compiler_params=small_params(1),
        )(block)

    slots = suffix_keys.shape[0] * suffix_keys.shape[1]
    slot_keys = suffix_keys.reshape(slots, -1)
    slot_values = suffix_values.reshape(slots, -1)

    token_blocks = gather_pairs(spread("spread", tokens))
    fresh_rows = 4 * KV_HEADS
    query_rows = samples * (width // HEAD_DIM)
    sent, cosine, sine = pl.pallas_call(
        functools.partial(project_kernel, prefix_tokens=prefix_keys.shape[0] * devices),
        name="project",
        cost_estimate=pl.CostEstimate(flops=40000000000, bytes_accessed=1000, transcendentals=0),
        out_shape=[
            jax.ShapeDtypeStruct((devices, query_rows + fresh_rows, HEAD_DIM), jnp.bfloat16),
            jax.ShapeDtypeStruct((samples, HEAD_DIM), jnp.float32),
            jax.ShapeDtypeStruct((samples, HEAD_DIM), jnp.float32),
        ],
        in_specs=[whole(SMEM)] + [whole(VMEM)] * 6,
        out_specs=[whole(VMEM)] * 3,
        scratch_shapes=[
            VMEM((devices, samples, width), jnp.bfloat16),
            VMEM((samples, fresh_rows // 2, HEAD_DIM), jnp.float32),
        ],
        compiler_params=small_params(4),
    )(suffix_lengths, *token_blocks, attn_gain, q_weight, k_weight, v_weight)
    query_blocks = exchange(sent)
    sent, suffix_sum, suffix_stat = pl.pallas_call(
        attend_kernel,
        name="attend",
        cost_estimate=pl.CostEstimate(flops=40000000000, bytes_accessed=1000, transcendentals=0),
        out_shape=[
            jax.ShapeDtypeStruct((samples, HEADS + STAT_ROWS, HEAD_DIM), jnp.bfloat16),
            jax.ShapeDtypeStruct((HEADS, HEAD_DIM), jnp.float32),
            jax.ShapeDtypeStruct((STAT_ROWS, HEADS), jnp.float32),
        ],
        in_specs=[whole(SMEM)] * 2 + [whole(VMEM)] * 7,
        out_specs=[whole(VMEM)] * 3,
        scratch_shapes=[
            VMEM((samples, HEADS, HEAD_DIM), jnp.float32),
            VMEM((samples, HEADS, HEAD_DIM), jnp.float32),
        ],
        compiler_params=small_params(4),
    )(
        suffix_lengths, suffix_table, query_blocks, cosine, sine,
        prefix_keys, prefix_values, slot_keys, slot_values,
    )
    part_blocks = exchange(sent)
    sent = pl.pallas_call(
        merge_kernel,
        name="merge",
        cost_estimate=pl.CostEstimate(flops=40000000000, bytes_accessed=1000, transcendentals=0),
        out_shape=jax.ShapeDtypeStruct((devices // 2, HEADS, HEAD_DIM), jnp.bfloat16),
        in_specs=[whole(VMEM)] * 3,
        out_specs=whole(VMEM),
        scratch_shapes=[VMEM((devices, STAT_ROWS, HEAD_DIM), jnp.float32)],
        compiler_params=small_params(3),
    )(part_blocks, suffix_sum, suffix_stat)
    attention = gather_pairs(sent)
    mixed = pl.pallas_call(
        output_kernel,
        name="output",
        cost_estimate=pl.CostEstimate(flops=40000000000, bytes_accessed=1000, transcendentals=0),
        out_shape=jax.ShapeDtypeStruct(tokens.shape, jnp.bfloat16),
        in_specs=[whole(VMEM)] * 4,
        out_specs=whole(VMEM),
        scratch_shapes=[VMEM((samples, HEADS, HEAD_DIM), jnp.float32)],
        compiler_params=small_params(3),
    )(*attention, tokens, o_weight)
    mixed_blocks = gather_pairs(spread("spread_mixed", mixed))
    pair_shape = (devices // 2,) + tokens.shape
    own_sums, other_sums = pl.pallas_call(
        feed_kernel,
        name="feed",
        out_shape=[
            jax.ShapeDtypeStruct(pair_shape, jnp.float32),
            jax.ShapeDtypeStruct(pair_shape, jnp.bfloat16),
        ],
        in_specs=[whole(VMEM)] * 6,
        out_specs=[whole(VMEM)] * 2,
        compiler_params=small_params(3),
    )(*mixed_blocks, mlp_gain, gate_weight, up_weight, down_weight)
    sent = pl.pallas_call(
        pair_kernel,
        name="pair",
        out_shape=jax.ShapeDtypeStruct(pair_shape, jnp.bfloat16),
        in_specs=[whole(VMEM)] * 2,
        out_specs=whole(VMEM),
        compiler_params=small_params(1),
    )(own_sums, swap_cores(other_sums))
    shares = jnp.sum(exchange_like_cores(sent).astype(jnp.float32), axis=0)
    return (mixed.astype(jnp.float32) + shares).astype(jnp.bfloat16)


def fits_kernels(devices, args):
    tokens, k_weight, suffix_table = args[0], args[4], args[15]
    samples, width = tokens.shape
    return (
        width % HEAD_DIM == 0
        and HEADS % devices == 0
        and (HEADS // KV_HEADS) % (HEADS // devices) == 0
        and suffix_table.shape[0] == 1
        and samples == devices
        and devices % 2 == 0
        and samples % 16 == 0
        and k_weight.shape[0] == width
    )


def choose_body(*args):
    if fits_kernels(lax.axis_size("ctx"), args):
        return kernel_body(*args)
    return body(*args)


def solution(mesh):
    placed = (
        P("groups", "ctx"),
        P(),
        P(),
        P(None, "ctx"),
        P("ctx", None),
        P("ctx", None),
        P(None, "ctx"),
        P(None, "ctx"),
        P(None, "ctx"),
        P("ctx", None),
        P(("groups", "ctx"), None),
        P(("groups", "ctx"), None),
        P(("groups", "ctx"), None, None),
        P(("groups", "ctx"), None, None),
        P("groups"),
        P(("groups", "ctx"), None),
    )
    return jax.shard_map(
        choose_body, mesh=mesh, in_specs=placed, out_specs=P("groups", "ctx"), check_vma=False
    )
```
